32 devices in a mesh: ctx: 8 (over z, x), head: 4 (over y, core).
Axes of the slice: x: 2, y: 2, z: 4, core: 2. Of those that a mesh axis runs over, the one named last changes fastest.
Arguments:
- x_load: bfloat16 [4096, 8192], P('ctx', 'head'), may hold values from -6 to 6
- bc_load: bfloat16 [4096, 256], P('ctx'), may hold values from -0.59765625 to 0.59765625
- dt_load: bfloat16 [4096, 128], P('ctx', 'head'), may hold values from 0.34960938 to 2.796875
- decay_rate: float32 [128], P('head'), may hold values from 6.1035156e-05 to 0.02
- doc_ids: int32 [4096], P('ctx'), may hold values from 0 to 3, never falling along the last dimension, each value on 1 to 3072 neighbouring positions
- destination: int32 [4096], replicated, may hold values from 0 to 4095, as said below
- grad_y: bfloat16 [4096, 8192], P('ctx', 'head'), may hold values from -6 to 6
Outputs:
- scan_output: bfloat16 [4096, 8192], P('ctx', 'head')
- dx_load: bfloat16 [4096, 8192], P('ctx', 'head')
- dbc_load: bfloat16 [4096, 256], P('ctx')
- ddt_load: bfloat16 [4096, 128], P('ctx', 'head')
The draws below stay inside these ranges and needn't reach their ends.
Inputs may be any that keep to these rules, and one draw needn't show every extreme that they name: `destination`: a permutation of the 4096 context positions; the rows of one loader device (aligned blocks of 512 rows) send at most 128 rows to the positions of one context device, and some pairs of devices reach 128. `doc_ids`: never falling along the positions; each document is 1 to 3072 positions long, one exactly 3072.
All inputs are finite; a program needn't handle non-finite values.
Results may differ from the reference program's by a relative error of at most 0.001.
Values may be sent and summed in bfloat16 or wider, within the bound.
No kernel may reach another device: no remote copies, remote signals or barrier semaphores. Data moves between devices by JAX's collectives and lax.ppermute only.
A program may use at most 192 MiB of HBM per device.

```python
import math
import jax
import jax.numpy as jnp
import numpy as np
from jax import lax

HEADS = 128
HEAD_DIM = 64
STATE = 128
BLOCK = 256
TOK_DEV = 512
TOKENS = 4096
CHANNELS = 8192
SLOTS = 128
DOCS = 4
DOC_MOST = 3072


def draw_destination(key, part):
    shards = TOKENS // TOK_DEV
    quarter = shards // 4
    counts = jnp.concatenate([jnp.full((quarter,), SLOTS, jnp.int32), jnp.full((shards - 2 * quarter,), SLOTS // 2, jnp.int32), jnp.zeros((quarter,), jnp.int32)])
    key_a, key_b, key_c, key_d = jax.random.split(key, 4)
    pattern = jax.random.permutation(key_a, counts)
    offset = jax.random.randint(key_b, (), 0, shards)
    source_idx = jnp.arange(shards, dtype=jnp.int32)[:, None]
    target_idx = jnp.arange(shards, dtype=jnp.int32)[None, :]
    matrix = pattern[(target_idx - source_idx + offset) % shards]
    out_end = jnp.cumsum(matrix, axis=1).astype(jnp.int32)
    out_start = out_end - matrix
    in_start = (jnp.cumsum(matrix, axis=0) - matrix).astype(jnp.int32)
    ordinal = jnp.arange(TOK_DEV, dtype=jnp.int32)
    target = jnp.sum((out_end[:, None, :] <= ordinal[None, :, None]).astype(jnp.int32), axis=2).astype(jnp.int32)
    starts = jnp.take_along_axis(out_start, target, axis=1)
    arrival = jnp.take_along_axis(in_start, target, axis=1)
    sequence = (arrival + ordinal[None, :] - starts).astype(jnp.int32)
    place_keys = jax.random.split(key_c, shards)
    place_perm = jax.vmap(lambda one_key: jax.random.permutation(one_key, TOK_DEV))(place_keys).astype(jnp.int32)
    position = target * TOK_DEV + place_perm[target, sequence]
    row_keys = jax.random.split(key_d, shards)
    row_perm = jax.vmap(lambda one_key: jax.random.permutation(one_key, TOK_DEV))(row_keys).astype(jnp.int32)
    flat_rows = (jnp.arange(shards, dtype=jnp.int32)[:, None] * TOK_DEV + row_perm).reshape(-1)
    result = jnp.zeros((TOKENS,), jnp.int32).at[flat_rows].set(position.reshape(-1).astype(jnp.int32))
    return result


def level_of(stream_key, shape, cuts, least, high):
    gain, own = 1.0, jax.random.fold_in(stream_key, 6)
    for dim, blocks in cuts:
        draws = jnp.exp(jax.random.uniform(jax.random.fold_in(own, dim), (blocks,), jnp.float32, least / len(cuts), high / len(cuts)))
        gain = gain * jnp.repeat(draws, shape[dim] // blocks).reshape([-1 if axis == dim else 1 for axis in range(len(shape))])
    return gain


def split_up(amount, total, bound, lean):
    weights = [(1 << 20) // math.isqrt(grade ** lean) + 1 for grade in range(2, amount + 1)]
    spare, holding = total - bound - (amount - 1), [1] * (amount - 1)
    while spare > 0:
        free = [i for i in range(amount - 1) if holding[i] < bound]
        pool, left = sum([weights[i] for i in free]), spare
        for i in free:
            addition = min(bound - holding[i], max(1, left * weights[i] // pool), spare)
            holding[i] = holding[i] + addition
            spare = spare - addition
    return np.array([bound] + holding)


def uneven_parts(rng, number_of, total, bound, skew):
    if number_of == 2:
        one = jax.random.randint(rng, (), max(1, total - bound), min(bound, total - 1) + 1)
        return jnp.stack([one, total - one])
    lengths = jnp.asarray(split_up(number_of, total, bound, skew), jnp.int32)
    pairs = (number_of - 1) // 2
    source_of, sink = lengths[1:1 + 2 * pairs:2], lengths[2:2 + 2 * pairs:2]
    room = jnp.minimum(source_of - 1, bound - sink)
    shifted = jax.random.randint(jax.random.fold_in(rng, 1), (pairs,), 0, 1 << 20) % (room + 1)
    lengths = lengths.at[1:1 + 2 * pairs:2].set(source_of - shifted).at[2:2 + 2 * pairs:2].set(sink + shifted)
    return lengths[jax.random.permutation(jax.random.fold_in(rng, 2), number_of)]


def scatter_about(rng, extent, deviation, limit, cuts=(), kind=jnp.bfloat16):
    array = deviation * jax.random.normal(rng, extent, jnp.float32)
    if cuts:
        array = array * level_of(rng, extent, cuts, -0.22, 0.18)
    return jnp.clip(array, -limit, limit).astype(kind)


def setup_inputs(seed: int = 0) -> dict:
    seeds = jax.random.split(jax.random.key(seed), 8)
    return {
        "x_load": scatter_about(seeds[0], (TOKENS, CHANNELS), 1.0, 6.0, ((0, 8), (1, 4))),
        "bc_load": scatter_about(seeds[1], (TOKENS, 2 * STATE), 0.1, 0.59765625, ((0, 8),)),
        "dt_load": jnp.clip(jnp.exp(math.log(2.796875) - 2.0794415 * jax.random.uniform(seeds[2], (TOKENS, HEADS), jnp.float32) ** level_of(seeds[2], (TOKENS, HEADS), ((0, 8), (1, 4)), -0.2, 0.2)), 0.34960938, 2.796875).astype(jnp.bfloat16),
        "decay_rate": jnp.clip(jnp.exp(math.log(0.02) - 5.7920375 * jax.random.uniform(seeds[3], (HEADS,), jnp.float32) ** level_of(seeds[3], (HEADS,), ((0, 4),), -0.2, 0.2)), 6.103515625e-05, 0.02),
        "doc_ids": jnp.searchsorted(jnp.cumsum(uneven_parts(seeds[4], DOCS, TOKENS, DOC_MOST, 2)), jnp.arange(TOKENS), side="right").astype(jnp.int32),
        "destination": draw_destination(jax.random.fold_in(seeds[7], 71), 0),
        "grad_y": scatter_about(seeds[6], (TOKENS, CHANNELS), 1.0, 6.0, ((0, 8), (1, 4))),
    }


PRECISE = lax.Precision.HIGHEST

def head_forward(x_head, b_rows, c_rows, dt_head, head_rate, doc_list):
    block_count = x_head.shape[0] // BLOCK
    log_decay = (-head_rate * dt_head).reshape(block_count, BLOCK)
    running = jnp.cumsum(log_decay, axis=1)
    totals = running[:, -1]
    scaled = (dt_head[:, None] * x_head).reshape(block_count, BLOCK, -1)
    b_blocks = b_rows.reshape(block_count, BLOCK, -1)
    c_blocks = c_rows.reshape(block_count, BLOCK, -1)
    doc_blocks = doc_list.reshape(block_count, BLOCK)
    positions = jnp.arange(BLOCK, dtype=jnp.int32)
    lower_tri = positions[:, None] >= positions[None, :]
    same_doc = (doc_blocks[:, :, None] == doc_blocks[:, None, :]) & lower_tri[None]
    log_gaps = running[:, :, None] - running[:, None, :]
    weights = jnp.where(same_doc, jnp.exp(jnp.where(same_doc, log_gaps, 0.0)), 0.0)
    affinity = jnp.einsum('kin,kjn->kij', c_blocks, b_blocks, precision=PRECISE)
    y_local = jnp.einsum('kij,kjp->kip', affinity * weights, scaled, precision=PRECISE)
    leave_w = jnp.where(doc_blocks == doc_blocks[:, -1:], jnp.exp(totals[:, None] - running), 0.0)
    block_states = jnp.einsum('kj,kjn,kjp->knp', leave_w, b_blocks, scaled, precision=PRECISE)
    doc_prev = jnp.concatenate([jnp.full((1,), -1, jnp.int32), doc_blocks[:-1, -1].astype(jnp.int32)])
    carry_k = jnp.exp(totals) * (doc_blocks[:, -1] == doc_prev).astype(jnp.float32)

    def chain_step(carried, pieces):
        factor, fresh_state = pieces
        return (factor * carried + fresh_state, carried)
    start_state = jnp.zeros((b_rows.shape[1], x_head.shape[1]), jnp.float32)
    _, entering = lax.scan(chain_step, start_state, (carry_k, block_states))
    enter_w = jnp.where(doc_blocks == doc_prev[:, None], jnp.exp(running), 0.0)
    y_cross = enter_w[:, :, None] * jnp.einsum('kin,knp->kip', c_blocks, entering, precision=PRECISE)
    return (y_local + y_cross).reshape(x_head.shape)

def reference(x_load, bc_load, dt_load, decay_rate, doc_ids, destination, grad_y):
    x_ctx = jnp.zeros_like(x_load).at[destination].set(x_load)
    bc_ctx = jnp.zeros_like(bc_load).at[destination].set(bc_load)
    dt_ctx = jnp.zeros_like(dt_load).at[destination].set(dt_load)
    b_rows = bc_ctx[:, :STATE].astype(jnp.float32)
    c_rows = bc_ctx[:, STATE:].astype(jnp.float32)
    x_heads = x_ctx.reshape(TOKENS, HEADS, HEAD_DIM).transpose(1, 0, 2)
    dy_heads = grad_y.reshape(TOKENS, HEADS, HEAD_DIM).transpose(1, 0, 2)
    dt_heads = dt_ctx.T

    def per_head(sums, pieces):
        x_head, dy_head, dt_head, head_rate = pieces

        def forward(x_part, b_part, c_part, dt_part):
            return head_forward(x_part, b_part, c_part, dt_part, head_rate, doc_ids)
        y_head, pullback = jax.vjp(forward, x_head.astype(jnp.float32), b_rows, c_rows, dt_head.astype(jnp.float32))
        grad_x, grad_b, grad_c, grad_dt = pullback(dy_head.astype(jnp.float32))
        return ((sums[0] + grad_b, sums[1] + grad_c), (y_head.astype(jnp.bfloat16), grad_x.astype(jnp.bfloat16), grad_dt.astype(jnp.bfloat16)))
    empty_sum = jnp.zeros((TOKENS, STATE), jnp.float32)
    (grad_b_all, grad_c_all), (y_all, grad_x_all, grad_dt_all) = lax.scan(per_head, (empty_sum, empty_sum), (x_heads, dy_heads, dt_heads, decay_rate))
    scan_output = y_all.transpose(1, 0, 2).reshape(TOKENS, CHANNELS)
    grad_x_ctx = grad_x_all.transpose(1, 0, 2).reshape(TOKENS, CHANNELS)
    grad_bc_ctx = jnp.concatenate([grad_b_all, grad_c_all], axis=1).astype(jnp.bfloat16)
    grad_dt_ctx = grad_dt_all.T
    return (scan_output, grad_x_ctx[destination], grad_bc_ctx[destination], grad_dt_ctx[destination])
```

```python
import functools
import jax
import jax.numpy as jnp
from jax import lax
from jax.experimental import pallas as pl
from jax.experimental.pallas import tpu as pltpu
from jax.sharding import PartitionSpec as P

BLOCK = 256
F32, BF16, I32 = jnp.float32, jnp.bfloat16, jnp.int32
NN, NT, TN = (((1,), (0,)), ((), ())), (((1,), (1,)), ((), ())), (((0,), (0,)), ((), ()))
VMEM = pl.BlockSpec(memory_space=pltpu.VMEM)
SMEM = pl.BlockSpec(memory_space=pltpu.SMEM)


def dot(a, b, dims=NN):
    return lax.dot_general(a, b, dims, preferred_element_type=F32)


def split2(v):
    hi = v.astype(BF16)
    return hi, (v - hi.astype(F32)).astype(BF16)


def dot2(a, b, dims=NN):
    if isinstance(a, tuple):
        return dot(a[0], b, dims) + dot(a[1], b, dims)
    return dot(a, b[0], dims) + dot(a, b[1], dims)


def dot3(a, b, dims=NN):
    return dot(a[0], b[0], dims) + (dot(a[0], b[1], dims) + dot(a[1], b[0], dims))


def column(row):
    return jnp.broadcast_to(row.astype(F32), (128, row.shape[1])).T[:, :1]


def expander(heads, width, head_dim):
    h = lax.broadcasted_iota(I32, (heads, width), 0)
    c = lax.broadcasted_iota(I32, (heads, width), 1)
    return jnp.where(c // head_dim == h, 1.0, 0.0).astype(BF16)


def place_kernel(pieces, head_dim, dest_ref, dt_ref, *refs):
    bc_refs, (bc_out, dt_out) = refs[:pieces], refs[pieces:]
    size = bc_refs[0].shape[0]
    first = pl.program_id(0) * BLOCK
    acc_bc = jnp.zeros((BLOCK, bc_out.shape[1]), F32)
    acc_dt = jnp.zeros((BLOCK, dt_ref.shape[0]), F32)
    for e in range(pieces):
        here = lax.broadcasted_iota(I32, (BLOCK, size), 0) + first
        pick = jnp.where(here == dest_ref[:, e * size : (e + 1) * size], 1.0, 0.0).astype(BF16)
        acc_bc = acc_bc + dot(pick, bc_refs[e][...])
        acc_dt = acc_dt + dot(pick, dt_ref[:, e * size : (e + 1) * size], NT)
    bc_out[...] = acc_bc.astype(BF16)
    spread = expander(dt_ref.shape[0], dt_out.shape[1], head_dim)
    dt_out[...] = dot(acc_dt.astype(BF16), spread).astype(BF16)


def decays(dt_ref, rate_ref):
    rows = lax.broadcasted_iota(I32, (BLOCK, BLOCK), 0)
    cols = lax.broadcasted_iota(I32, (BLOCK, BLOCK), 1)
    lower = jnp.where(rows >= cols, 1.0, 0.0).astype(BF16)
    running = rate_ref[...] * dot(lower, dt_ref[...])
    return jnp.exp(-running), jnp.exp(running), jnp.exp(-running[BLOCK - 1 :, :])


def doc_state(doc_smem, block):
    last = doc_smem[block * BLOCK + BLOCK - 1]
    prev = jnp.where(block == 0, -1.0, doc_smem[jnp.maximum(block * BLOCK - 1, 0)])
    return prev, last


def back_kernel(
    blocks, doc_smem, doc_ref, dest_ref, rate_ref, bc_ref, dt_ref, dy_ref,
    du_out, grad_out, dx_out, grad_ref, dx_ref,
):
    step = pl.program_id(0)

    @pl.when(step == 0)
    def _():
        grad_ref[...] = jnp.zeros_like(grad_ref)

    @pl.when(step < blocks)
    def _():
        block = blocks - 1 - step
        b, c = bc_ref[:, :128], bc_ref[:, 128:]
        enter, leave, total = decays(dt_ref, rate_ref)
        prev, last = doc_state(doc_smem, block)
        row = doc_ref[...]
        col = column(row)
        rows = lax.broadcasted_iota(I32, (BLOCK, BLOCK), 0)
        cols = lax.broadcasted_iota(I32, (BLOCK, BLOCK), 1)
        later = (col == row) & (cols >= rows)
        affinity = split2(jnp.where(later, dot(b, c, NT), 0.0))
        dy = split2(enter * dy_ref[...].astype(F32))
        grad = grad_ref[...]
        grad_out[0] = grad
        carried = total * grad
        b_last = jnp.where(col == last, b.astype(F32), 0.0).astype(BF16)
        c_first = jnp.where(col == prev, c.astype(F32), 0.0).astype(BF16)
        du = leave * (dot3(affinity, dy) + dot2(b_last, split2(carried)))
        du_out[...] = du
        dx_ref[pl.ds(pl.multiple_of(block * BLOCK, BLOCK), BLOCK), :] = (
            dt_ref[...].astype(F32) * du
        ).astype(BF16)
        grad_ref[...] = jnp.where(prev == last, carried, 0.0) + dot2(c_first, dy, TN)

    @pl.when(step >= blocks)
    def _():
        want = column(dest_ref[...]).astype(I32)
        tokens = dx_ref.shape[0]
        here = lax.broadcasted_iota(I32, (BLOCK, tokens), 1)
        pick = jnp.where(here == want, 1.0, 0.0).astype(BF16)
        dx_out[...] = dot(pick, dx_ref[...]).astype(BF16)


def front_kernel(
    blocks, head_dim, doc_smem, dest_smem, doc_ref, dest_ref, x_ref, rate_ref, rate_col,
    bc_ref, dt_ref, dy_ref, du_ref, grad_ref,
    y_out, dbc_out, ddt_out, state_ref, sum_ref, dbc_ref, ddt_ref,
):
    step = pl.program_id(0)

    @pl.when(step == 0)
    def _():
        state_ref[...] = jnp.zeros_like(state_ref)
        sum_ref[...] = jnp.zeros_like(sum_ref)

    @pl.when(step < blocks)
    def _():
        block = step
        tokens, width = x_ref.shape
        here = lax.broadcasted_iota(I32, (BLOCK, tokens), 0) + block * BLOCK
        pick = jnp.where(here == dest_ref[...], 1.0, 0.0).astype(BF16)
        x = dot(pick, x_ref[...])
        b, c = bc_ref[:, :128], bc_ref[:, 128:]
        enter, leave, total = decays(dt_ref, rate_ref)
        prev, last = doc_state(doc_smem, block)
        row = doc_ref[...]
        col = column(row)
        rows = lax.broadcasted_iota(I32, (BLOCK, BLOCK), 0)
        cols = lax.broadcasted_iota(I32, (BLOCK, BLOCK), 1)
        same = col == row
        earlier = same & (rows >= cols)
        affinity = split2(jnp.where(earlier, dot(c, b, NT), 0.0))
        dy_now = dy_ref[...].astype(F32)
        dy = split2(enter * dy_now)
        scaled = dt_ref[...].astype(F32) * x
        ux = split2(leave * scaled)
        is_last, is_first = col == last, col == prev
        b_last = jnp.where(is_last, b.astype(F32), 0.0).astype(BF16)
        c_first = jnp.where(is_first, c.astype(F32), 0.0).astype(BF16)
        state = state_ref[...]
        state2 = split2(state)
        y = enter * (dot3(affinity, ux) + dot2(c_first, state2))
        y_out[...] = y.astype(BF16)
        state_ref[...] = total * (jnp.where(prev == last, state, 0.0) + dot2(b_last, ux, TN))
        pairs = split2(jnp.where(earlier, dot3(dy, ux, NT), 0.0))
        grad2 = split2(total * grad_ref[0])
        dc = dot2(pairs, b) + jnp.where(is_first, dot3(dy, state2, NT), 0.0)
        db = dot2(pairs, c, TN) + jnp.where(is_last, dot3(ux, grad2, NT), 0.0)
        here_rows = pl.ds(pl.multiple_of(block * BLOCK, BLOCK), BLOCK)
        dbc_ref[here_rows, :128] = db
        dbc_ref[here_rows, 128:] = dc
        du = du_ref[...]
        heads = sum_ref.shape[0]
        spread = expander(heads, width, head_dim)

        def by_head(v):
            hi, low = split2(v)
            rest = (v - hi.astype(F32) - low.astype(F32)).astype(BF16)
            return dot(spread, hi, NT) + dot(spread, low, NT) + dot(spread, rest, NT)

        balance = by_head(scaled * du - dy_now * y)
        hi, low = split2(balance)
        rest = (balance - hi.astype(F32) - low.astype(F32)).astype(BF16)
        before = jnp.where(same & (rows < cols), 1.0, 0.0).astype(BF16)
        prefix = dot(hi, before) + dot(low, before) + dot(rest, before)
        prefix = prefix + jnp.where(row == prev, sum_ref[:, :1], 0.0)
        sum_ref[...] = jnp.broadcast_to(
            prefix[:, BLOCK - 1 :] + balance[:, BLOCK - 1 :], sum_ref.shape
        )
        ddt = by_head(x * du) - rate_col[...] * prefix
        ddt = jnp.concatenate([ddt, jnp.zeros((128 - heads, BLOCK), F32)], axis=0)
        ddt_ref[here_rows, :] = ddt.T

    @pl.when(step >= blocks)
    def _():
        base = (step - blocks) * BLOCK

        def rows8(i, carry):
            at = pl.multiple_of(i * 8, 8)
            spots = [dest_smem[base + at + j] for j in range(8)]
            dbc_out[pl.ds(at, 8), :] = jnp.concatenate(
                [dbc_ref[pl.ds(s, 1), :] for s in spots], axis=0
            )
            small[pl.ds(at, 8), :] = jnp.concatenate(
                [ddt_ref[pl.ds(s, 1), :] for s in spots], axis=0
            )
            return carry

        def run(buffer):
            nonlocal small
            small = buffer
            lax.fori_loop(0, BLOCK // 8, rows8, 0, unroll=4)
            ddt_out[...] = buffer[...].T[: ddt_out.shape[0], :]

        small = None
        pl.run_scoped(run, pltpu.VMEM((BLOCK, 128), F32))


def params(**extra):
    return pltpu.CompilerParams(
        dimension_semantics=("arbitrary",), vmem_limit_bytes=60 << 20, **extra
    )


def body(x_load, bc_load, dt_load, decay_rate, doc_ids, destination, grad_y):
    shards, teams = lax.axis_size("ctx"), lax.axis_size("head")
    me, team = lax.axis_index("ctx"), lax.axis_index("head")
    rows_dev, chan_dev = x_load.shape
    heads_dev = dt_load.shape[1]
    head_dim = chan_dev // heads_dev
    width = chan_dev // shards
    tokens = rows_dev * shards
    blocks = tokens // BLOCK
    heads = max(1, width // head_dim)
    sharing = shards * heads // heads_dev
    padded = -(-heads // 8) * 8
    quarter = rows_dev // teams

    def exchange(v):
        return lax.all_to_all(v, "ctx", split_axis=0, concat_axis=0, tiled=True)

    def by_channel(v):
        parts = v.reshape(rows_dev, shards, width).transpose(1, 0, 2)
        return exchange(parts.reshape(tokens, width))

    own_bc = lax.dynamic_slice_in_dim(bc_load, team * quarter, quarter)
    sent_bc = jnp.broadcast_to(own_bc[None], (shards,) + own_bc.shape)
    part_bc = exchange(sent_bc.reshape(shards * quarter, -1))
    head_of = jnp.asarray([[k * width // head_dim + h for h in range(heads)] for k in range(shards)])
    dt_rows = dt_load.T[head_of]
    doc_rows = jnp.broadcast_to(doc_ids.astype(BF16)[None, None], (shards, 1, rows_dev))
    small = exchange(jnp.concatenate([dt_rows, doc_rows], axis=1).reshape(-1, rows_dev))
    small = small.reshape(shards, heads + 1, rows_dev)
    docs = small[:, heads].astype(F32).reshape(tokens)
    dt_all = small[:, :heads].transpose(1, 0, 2).reshape(heads, tokens)
    pieces = [part_bc]
    for e in range(1, teams):
        pieces.append(lax.ppermute(part_bc, "head", [(i, i ^ e) for i in range(teams)]))
    order = jnp.stack([team ^ e for e in range(teams)])
    dest_bc = jnp.take(destination.reshape(shards, teams, quarter), order, axis=1)
    dest_bc = dest_bc.transpose(1, 0, 2).reshape(1, tokens)
    dt_bc = jnp.take(dt_all.reshape(heads, shards, teams, quarter), order, axis=2)
    dt_bc = dt_bc.transpose(0, 2, 1, 3).reshape(heads, tokens)
    dt_bc = jnp.concatenate([dt_bc, jnp.zeros((16 - heads, tokens), BF16)], axis=0)

    dy_all = by_channel(grad_y)
    x_all = by_channel(x_load)

    rate_here = lax.dynamic_slice_in_dim(decay_rate, me * width // head_dim, heads)
    rate_row = jnp.repeat(rate_here, width // heads)[None]
    rate_col = jnp.concatenate([rate_here, jnp.zeros((padded - heads,), F32)])[:, None]
    dest_row, doc_row = destination[None], docs[None]

    def blocked(cols, index):
        return pl.BlockSpec((BLOCK, cols), lambda s: (index(s), 0))

    def rowed(rows, index):
        return pl.BlockSpec((rows, BLOCK), lambda s: (0, index(s)))

    bc_ctx, dt_ctx = pl.pallas_call(
        functools.partial(place_kernel, teams, head_dim),
        grid=(blocks,),
        in_specs=[VMEM] * (2 + teams),
        out_specs=[blocked(256, lambda s: s), blocked(width, lambda s: s)],
        out_shape=[
            jax.ShapeDtypeStruct((tokens, 256), BF16),
            jax.ShapeDtypeStruct((tokens, width), BF16),
        ],
        compiler_params=params(),
        cost_estimate=pl.CostEstimate(
            flops=2 * tokens * tokens * 384, bytes_accessed=tokens * 1600, transcendentals=0
        ),
        name="place",
    )(dest_bc, dt_bc, *pieces)

    down = lambda s: jnp.maximum(blocks - 1 - s, 0)
    after = lambda s: jnp.maximum(s - blocks, 0)
    up = lambda s: jnp.minimum(s, blocks - 1)
    du, grads, dx_sent = pl.pallas_call(
        functools.partial(back_kernel, blocks),
        grid=(2 * blocks,),
        in_specs=[
            SMEM, rowed(1, down), rowed(1, after), VMEM,
            blocked(256, down), blocked(width, down), blocked(width, down),
        ],
        out_specs=[
            blocked(width, down),
            pl.BlockSpec((1, 128, width), lambda s: (down(s), 0, 0)),
            blocked(width, after),
        ],
        out_shape=[
            jax.ShapeDtypeStruct((tokens, width), F32),
            jax.ShapeDtypeStruct((blocks, 128, width), F32),
            jax.ShapeDtypeStruct((tokens, width), BF16),
        ],
        scratch_shapes=[pltpu.VMEM((128, width), F32), pltpu.VMEM((tokens, width), BF16)],
        compiler_params=params(),
        cost_estimate=pl.CostEstimate(
            flops=2 * tokens * (tokens + 2000) * width,
            bytes_accessed=tokens * 3500,
            transcendentals=2 * tokens * width,
        ),
        name="back",
    )(docs, doc_row, dest_row, rate_row, bc_ctx, dt_ctx, dy_all)

    y_sent, dbc_part, ddt_part = pl.pallas_call(
        functools.partial(front_kernel, blocks, head_dim),
        grid=(2 * blocks,),
        in_specs=[
            SMEM, SMEM, rowed(1, up), VMEM, VMEM, VMEM, VMEM,
            blocked(256, up), blocked(width, up), blocked(width, up), blocked(width, up),
            pl.BlockSpec((1, 128, width), lambda s: (up(s), 0, 0)),
        ],
        out_specs=[blocked(width, up), blocked(256, after), rowed(padded, after)],
        out_shape=[
            jax.ShapeDtypeStruct((tokens, width), BF16),
            jax.ShapeDtypeStruct((tokens, 256), F32),
            jax.ShapeDtypeStruct((padded, tokens), F32),
        ],
        scratch_shapes=[
            pltpu.VMEM((128, width), F32),
            pltpu.VMEM((padded, 128), F32),
            pltpu.VMEM((tokens, 256), F32),
            pltpu.VMEM((tokens, 128), F32),
        ],
        compiler_params=params(),
        cost_estimate=pl.CostEstimate(
            flops=2 * tokens * (tokens + 4000) * width,
            bytes_accessed=tokens * 6000,
            transcendentals=2 * tokens * width,
        ),
        name="front",
    )(docs, destination, doc_row, dest_row, x_all, rate_row, rate_col, bc_ctx, dt_ctx, dy_all, du, grads)

    def from_channel(v):
        got = exchange(v).reshape(shards, rows_dev, width)
        return got.transpose(1, 0, 2).reshape(rows_dev, chan_dev)

    dx_load = from_channel(dx_sent)

    part = dbc_part.reshape(shards, teams, quarter, 256)
    reach = 1
    while reach < teams:
        size = part.shape[1]
        folded = part.reshape(shards, size // 2, 2, quarter, 256)
        bit = (team // reach) % 2
        keep = lax.dynamic_index_in_dim(folded, bit, 2, False)
        give = lax.dynamic_index_in_dim(folded, 1 - bit, 2, False)
        part = keep + lax.ppermute(give, "head", [(i, i ^ reach) for i in range(teams)])
        reach *= 2
    got = exchange(part.reshape(shards * quarter, 256)).reshape(shards, quarter, 256)
    mine = jnp.sum(got, axis=0).astype(BF16)
    shares = [mine] + [
        lax.ppermute(mine, "head", [(i, i ^ e) for i in range(teams)]) for e in range(1, teams)
    ]
    dbc_load = jnp.take(jnp.stack(shares), order, axis=0).reshape(rows_dev, 256)

    scan_output = from_channel(y_sent)
    ddt = ddt_part[:heads].reshape(heads, shards, rows_dev).transpose(1, 0, 2)
    ddt = exchange(ddt.reshape(shards * heads, rows_dev))
    ddt = jnp.sum(ddt.reshape(heads_dev, sharing, rows_dev), axis=1)
    return (scan_output, dx_load, dbc_load, ddt.T.astype(BF16))


def solution(mesh):
    return jax.shard_map(
        body,
        mesh=mesh,
        in_specs=(
            P("ctx", "head"),
            P("ctx", None),
            P("ctx", "head"),
            P("head"),
            P("ctx"),
            P(),
            P("ctx", "head"),
        ),
        out_specs=(P("ctx", "head"), P("ctx", "head"), P("ctx", None), P("ctx", "head")),
        check_vma=False,
    )
```

```python
import functools
import jax
import jax.numpy as jnp
from jax import lax
from jax.experimental import pallas as pl
from jax.experimental.pallas import tpu as pltpu
from jax.sharding import PartitionSpec as P


BLOCK = 256
PLACE = 1024
F32, BF16, I32 = jnp.float32, jnp.bfloat16, jnp.int32
NN, NT, TN = (((1,), (0,)), ((), ())), (((1,), (1,)), ((), ())), (((0,), (0,)), ((), ()))
VMEM = pl.BlockSpec(memory_space=pltpu.VMEM)
SMEM = pl.BlockSpec(memory_space=pltpu.SMEM)


def dot(a, b, dims=NN):
    return lax.dot_general(a, b, dims, preferred_element_type=F32)


def split2(v):
    hi = v.astype(BF16)
    return hi, (v - hi.astype(F32)).astype(BF16)


def expander(heads, width, head_dim):
    h = lax.broadcasted_iota(I32, (heads, width), 0)
    c = lax.broadcasted_iota(I32, (heads, width), 1)
    return jnp.where(c // head_dim == h, 1.0, 0.0).astype(BF16)


def place_kernel(pieces, head_dim, dest_ref, dt_ref, *refs):
    bc_refs, (bc_out, dt_out) = refs[:pieces], refs[pieces:]
    size = bc_refs[0].shape[0]
    block = bc_out.shape[0]
    first = pl.program_id(0) * block
    acc_bc = jnp.zeros((block, bc_out.shape[1]), F32)
    acc_dt = jnp.zeros((block, dt_ref.shape[0]), F32)
    for e in range(pieces):
        here = lax.broadcasted_iota(I32, (block, size), 0) + first
        pick = jnp.where(here == dest_ref[:, e * size : (e + 1) * size], 1.0, 0.0).astype(BF16)
        acc_bc = acc_bc + dot(pick, bc_refs[e][...])
        acc_dt = acc_dt + dot(pick, dt_ref[:, e * size : (e + 1) * size], NT)
    bc_out[...] = acc_bc.astype(BF16)
    spread = expander(dt_ref.shape[0], dt_out.shape[1], head_dim)
    dt_out[...] = dot(acc_dt.astype(BF16), spread).astype(BF16)


def constants(lower_ref, spread_ref, head_dim):
    rows = lax.broadcasted_iota(I32, (BLOCK, BLOCK), 0)
    cols = lax.broadcasted_iota(I32, (BLOCK, BLOCK), 1)
    lower_ref[...] = jnp.where(rows >= cols, 1.0, 0.0).astype(BF16)
    if spread_ref is not None:
        width = spread_ref.shape[0] // 2
        c = lax.broadcasted_iota(I32, (width, 128), 0)
        h = lax.broadcasted_iota(I32, (width, 128), 1)
        one = jnp.where(c // head_dim == h, 1.0, 0.0).astype(BF16)
        spread_ref[...] = jnp.concatenate([one] * 2, axis=0)


def decays(dt_ref, rate_ref, lower_ref):
    running = rate_ref[...] * dot(lower_ref[...], dt_ref[...])
    return jnp.exp(-running), jnp.exp(running), jnp.exp(-running[BLOCK - 1 :, :])


def doc_state(doc_smem, block):
    last = doc_smem[block * BLOCK + BLOCK - 1]
    prev = jnp.where(block == 0, -1.0, doc_smem[jnp.maximum(block * BLOCK - 1, 0)])
    return prev, last


def only(cond, v):
    return jnp.where(cond, v.astype(F32), 0.0).astype(BF16)


def lanes(*parts):
    return jnp.concatenate(parts, axis=1)


def stack(*parts):
    return jnp.concatenate(parts, axis=0)


def fore_kernel(
    doc_smem, doc_ref, doc_col, dest_ref, x_ref, rate_ref, bc_ref, dt_ref,
    y_out, yf_out, x_out, state_out, state_ref, lower_ref,
):
    block = pl.program_id(0)

    @pl.when(block == 0)
    def _():
        state_ref[...] = jnp.zeros_like(state_ref)
        constants(lower_ref, None, None)

    tokens = x_ref.shape[0]
    here = lax.broadcasted_iota(I32, (BLOCK, tokens), 0) + block * BLOCK
    pick = jnp.where(here == dest_ref[...], 1.0, 0.0).astype(BF16)
    x = dot(pick, x_ref[...])
    x_out[...] = x.astype(BF16)
    b, c = bc_ref[:, :128], bc_ref[:, 128:]
    enter, leave, total = decays(dt_ref, rate_ref, lower_ref)
    prev, last = doc_state(doc_smem, block)
    row, col = doc_ref[...], doc_col[...]
    rows = lax.broadcasted_iota(I32, (BLOCK, BLOCK), 0)
    cols = lax.broadcasted_iota(I32, (BLOCK, BLOCK), 1)
    earlier = (col == row) & (rows >= cols)
    ah, al = split2(jnp.where(earlier, dot(c, b, NT), 0.0))
    uh, ul = split2(leave * (dt_ref[...].astype(F32) * x))
    state = state_ref[...]
    state_out[0] = state
    sh, sl = split2(state)
    c_first = only(col == prev, c)
    y = enter * dot(lanes(ah, ah, al, c_first, c_first), stack(uh, ul, uh, sh, sl))
    yf_out[...] = y
    y_out[...] = y.astype(BF16)
    b_last = only(col == last, b)
    fresh = dot(stack(b_last, b_last), stack(uh, ul), TN)
    state_ref[...] = total * (jnp.where(prev == last, state, 0.0) + fresh)


def back_kernel(
    blocks, head_dim, doc_smem, side_smem, doc_ref, doc_col, rate_ref, rate_lane,
    bc_ref, dt_ref, x_ref, dy_ref, y_ref, state_ref,
    dx_out, keep_out, give_out, ddt_out,
    grad_ref, sum_ref, lower_ref, spread_ref,
):
    step = pl.program_id(0)

    @pl.when(step == 0)
    def _():
        grad_ref[...] = jnp.zeros_like(grad_ref)
        sum_ref[...] = jnp.zeros_like(sum_ref)
        constants(lower_ref, spread_ref, head_dim)

    block = blocks - 1 - step
    b, c = bc_ref[:, :128], bc_ref[:, 128:]
    enter, leave, total = decays(dt_ref, rate_ref, lower_ref)
    prev, last = doc_state(doc_smem, block)
    row, col = doc_ref[...], doc_col[...]
    rows = lax.broadcasted_iota(I32, (BLOCK, BLOCK), 0)
    cols = lax.broadcasted_iota(I32, (BLOCK, BLOCK), 1)
    later = (col == row) & (cols >= rows)
    is_last, is_first = col == last, col == prev
    ah, al = split2(jnp.where(later, dot(b, c, NT), 0.0))
    dt = dt_ref[...].astype(F32)
    x = x_ref[...].astype(F32)
    dy = dy_ref[...].astype(F32)
    gh, gl = split2(enter * dy)
    uh, ul = split2(leave * (dt * x))
    grad = total * grad_ref[...]
    rh, rl = split2(grad)
    sh, sl = split2(state_ref[0])
    b_last, c_first = only(is_last, b), only(is_first, c)
    du = leave * dot(lanes(ah, ah, al, b_last, b_last), stack(gh, gl, gh, rh, rl))
    dx = dt * du
    dx_out[...] = dx.astype(BF16)
    fresh = dot(stack(c_first, c_first), stack(gh, gl), TN)
    grad_ref[...] = jnp.where(prev == last, grad, 0.0) + fresh
    g3, u3 = lanes(gh, gl, gh), lanes(uh, uh, ul)
    qh, qlow = split2(jnp.where(later, dot(u3, g3, NT), 0.0))
    dc = dot(stack(qh, qlow), stack(b, b), TN)
    dc = dc + jnp.where(is_first, dot(g3, lanes(sh, sh, sl), NT), 0.0)
    db = dot(lanes(qh, qlow), stack(c, c))
    db = db + jnp.where(is_last, dot(u3, lanes(rh, rl, rh), NT), 0.0)
    side = side_smem[0] == 0
    keep_out[...] = jnp.where(side, db, dc)
    give_out[...] = jnp.where(side, dc, db)
    spread = spread_ref[...]
    balance = dot(lanes(*split2(dy * y_ref[...] - x * dx)), spread)
    mask = jnp.where(later, 1.0, 0.0).astype(BF16)
    suffix = dot(lanes(mask, mask), stack(*split2(balance)))
    suffix = suffix + jnp.where(is_last, sum_ref[:1, :], 0.0)
    sum_ref[...] = jnp.broadcast_to(
        jnp.where(prev == doc_smem[block * BLOCK], suffix[:1, :], 0.0), sum_ref.shape
    )
    ddt_out[...] = dot(lanes(*split2(x * du)), spread) - rate_lane[...] * suffix


def pick8(dest_smem, source, target, base):
    def rows8(i, carry):
        at = pl.multiple_of(i * 8, 8)
        spots = [dest_smem[base + at + j] for j in range(8)]
        target[pl.ds(at, 8), :] = stack(*[source[pl.ds(s, 1), :] for s in spots])
        return carry

    lax.fori_loop(0, target.shape[0] // 8, rows8, 0, unroll=4)


def rows_kernel(dest_smem, keep_ref, more_ref, dbc_out, sum_ref):
    sum_ref[...] = keep_ref[...] + more_ref[...]
    pick8(dest_smem, sum_ref, dbc_out, 0)


def turn_kernel(dest_smem, ddt_ref, ddt_out, small_ref):
    pick8(dest_smem, ddt_ref, small_ref, pl.program_id(0) * BLOCK)
    ddt_out[...] = small_ref[...].T[: ddt_out.shape[0], :]


def gather_kernel(dest_col, dx_ref, dx_out):
    here = lax.broadcasted_iota(I32, (dx_out.shape[0], dx_ref.shape[0]), 1)
    pick = jnp.where(here == dest_col[...], 1.0, 0.0).astype(BF16)
    dx_out[...] = dot(pick, dx_ref[...]).astype(BF16)


def params(**extra):
    return pltpu.CompilerParams(
        dimension_semantics=("arbitrary",), vmem_limit_bytes=60 << 20, **extra
    )


def struct(dtype, *shape):
    return jax.ShapeDtypeStruct(shape, dtype)


def blocked(cols, index, size=BLOCK):
    return pl.BlockSpec((size, cols), lambda s: (index(s), 0))


def rowed(rows, index):
    return pl.BlockSpec((rows, BLOCK), lambda s: (0, index(s)))


def planes(width, index):
    return pl.BlockSpec((1, 128, width), lambda s: (index(s), 0, 0))


def place(dest_bc, dt_bc, pieces, width, head_dim):
    tokens = dest_bc.shape[1]
    same = lambda s: s
    return pl.pallas_call(
        functools.partial(place_kernel, len(pieces), head_dim),
        grid=(tokens // PLACE,),
        in_specs=[VMEM] * (2 + len(pieces)),
        out_specs=[blocked(256, same, PLACE), blocked(width, same, PLACE)],
        out_shape=[struct(BF16, tokens, 256), struct(BF16, tokens, width)],
        compiler_params=params(),
        cost_estimate=pl.CostEstimate(
            flops=2 * tokens * tokens * 384, bytes_accessed=tokens * 1600, transcendentals=0
        ),
        name="place",
    )(dest_bc, dt_bc, *pieces)


def fore(docs, destination, x_all, rate_row, bc_ctx, dt_ctx):
    tokens, width = x_all.shape
    blocks = tokens // BLOCK
    same = lambda s: s
    return pl.pallas_call(
        fore_kernel,
        grid=(blocks,),
        in_specs=[
            SMEM, rowed(1, same), blocked(1, same), VMEM, VMEM, VMEM,
            blocked(256, same), blocked(width, same),
        ],
        out_specs=[blocked(width, same)] * 3 + [planes(width, same)],
        out_shape=[
            struct(BF16, tokens, width),
            struct(F32, tokens, width),
            struct(BF16, tokens, width),
            struct(F32, blocks, 128, width),
        ],
        scratch_shapes=[pltpu.VMEM((128, width), F32), pltpu.VMEM((BLOCK, BLOCK), BF16)],
        compiler_params=params(),
        cost_estimate=pl.CostEstimate(
            flops=2 * tokens * (tokens + 2000) * width,
            bytes_accessed=tokens * 4000,
            transcendentals=2 * tokens * width,
        ),
        name="fore",
    )(docs, docs[None], docs[:, None], destination[None], x_all, rate_row, bc_ctx, dt_ctx)


def back(docs, side, rate_row, rate_lane, bc_ctx, dt_ctx, x_ctx, dy_all, y_all, states, head_dim):
    tokens, width = x_ctx.shape
    blocks = tokens // BLOCK
    down = lambda s: blocks - 1 - s
    return pl.pallas_call(
        functools.partial(back_kernel, blocks, head_dim),
        grid=(blocks,),
        in_specs=[
            SMEM, SMEM, rowed(1, down), blocked(1, down), VMEM, VMEM,
            blocked(256, down), blocked(width, down), blocked(width, down),
            blocked(width, down), blocked(width, down), planes(width, down),
        ],
        out_specs=[blocked(width, down)] + [blocked(128, down)] * 3,
        out_shape=[struct(BF16, tokens, width)] + [struct(F32, tokens, 128)] * 3,
        scratch_shapes=[
            pltpu.VMEM((128, width), F32),
            pltpu.VMEM((8, 128), F32),
            pltpu.VMEM((BLOCK, BLOCK), BF16),
            pltpu.VMEM((2 * width, 128), BF16),
        ],
        compiler_params=params(),
        cost_estimate=pl.CostEstimate(
            flops=2 * tokens * 4000 * width,
            bytes_accessed=tokens * 6000,
            transcendentals=2 * tokens * width,
        ),
        name="back",
    )(
        docs, side, docs[None], docs[:, None], rate_row, rate_lane,
        bc_ctx, dt_ctx, x_ctx, dy_all, y_all, states,
    )


def gather_rows(spots, keep, more):
    return pl.pallas_call(
        rows_kernel,
        in_specs=[SMEM, VMEM, VMEM],
        out_specs=VMEM,
        out_shape=struct(F32, spots.shape[0], 128),
        scratch_shapes=[pltpu.VMEM(keep.shape, F32)],
        compiler_params=pltpu.CompilerParams(vmem_limit_bytes=60 << 20),
        cost_estimate=pl.CostEstimate(
            flops=keep.size, bytes_accessed=keep.size * 12, transcendentals=0
        ),
        name="gather_rows",
    )(spots, keep, more)


def gather_turn(destination, ddt, heads):
    tokens = ddt.shape[0]
    padded = -(-heads // 8) * 8
    return pl.pallas_call(
        turn_kernel,
        grid=(tokens // BLOCK,),
        in_specs=[SMEM, VMEM],
        out_specs=rowed(padded, lambda s: s),
        out_shape=struct(F32, padded, tokens),
        scratch_shapes=[pltpu.VMEM((BLOCK, 128), F32)],
        compiler_params=params(),
        cost_estimate=pl.CostEstimate(
            flops=tokens * 256, bytes_accessed=tokens * 1000, transcendentals=0
        ),
        name="gather_turn",
    )(destination, ddt)


def gather_back(destination, dx_ctx, shards):
    tokens, width = dx_ctx.shape
    size = tokens // shards
    return pl.pallas_call(
        gather_kernel,
        grid=(shards,),
        in_specs=[blocked(1, lambda s: s, size), VMEM],
        out_specs=blocked(width, lambda s: s, size),
        out_shape=struct(BF16, tokens, width),
        compiler_params=params(),
        cost_estimate=pl.CostEstimate(
            flops=2 * tokens * tokens * width, bytes_accessed=tokens * 1500, transcendentals=0
        ),
        name="gather_back",
    )(destination[:, None], dx_ctx)


def after(value, *others):
    return lax.optimization_barrier((value,) + others)[0]


def body(x_load, bc_load, dt_load, decay_rate, doc_ids, destination, grad_y):
    shards, teams = lax.axis_size("ctx"), lax.axis_size("head")
    me, team = lax.axis_index("ctx"), lax.axis_index("head")
    rows_dev, chan_dev = x_load.shape
    heads_dev = dt_load.shape[1]
    head_dim = chan_dev // heads_dev
    width = chan_dev // shards
    tokens = rows_dev * shards
    heads = max(1, width // head_dim)
    sharing = shards * heads // heads_dev
    quarter = rows_dev // teams

    def exchange(v):
        return lax.all_to_all(v, "ctx", split_axis=0, concat_axis=0, tiled=True)

    def ring(v, reach):
        return lax.ppermute(v, "ctx", [(i, i ^ reach) for i in range(shards)])

    def across(v, reach):
        return lax.ppermute(v, "head", [(i, i ^ reach) for i in range(teams)])

    def by_channel(v):
        parts = v.reshape(rows_dev, shards, width).transpose(1, 0, 2)
        return parts.reshape(tokens, width)

    def from_channel(got):
        got = got.reshape(shards, rows_dev, width)
        return got.transpose(1, 0, 2).reshape(rows_dev, chan_dev)

    own_bc = lax.dynamic_slice_in_dim(bc_load, team * quarter, quarter)
    small = jnp.concatenate([dt_load.T, doc_ids.astype(BF16)[None]], axis=0)
    extra = small.size // 256
    fill = jnp.zeros((-extra % 16, 256), BF16)
    held = jnp.concatenate([own_bc, small.reshape(-1, 256), fill], axis=0)[None]
    came, reach = [me], shards // 2
    while reach >= 1:
        held = jnp.concatenate([held, ring(held, reach)], axis=0)
        came = came + [t ^ reach for t in came]
        reach //= 2
    came = jnp.stack(came)
    part_bc = held[:, :quarter].reshape(shards * quarter, 256)
    small = jnp.take(held[:, quarter : quarter + extra], inverse(came), axis=0)
    small = small.reshape(shards, heads_dev + 1, rows_dev)
    docs = small[:, heads_dev].astype(F32).reshape(tokens)
    dt_all = lax.dynamic_slice_in_dim(small, me * width // head_dim, heads, axis=1)
    pieces, order, reach = [part_bc], [team], teams // 2
    while reach >= 1:
        pieces = pieces + [across(v, reach) for v in pieces]
        order = order + [t ^ reach for t in order]
        reach //= 2
    order = jnp.stack(order)
    dest_bc = jnp.take(destination.reshape(shards, teams, quarter), order, axis=1)
    dest_bc = jnp.take(dest_bc, came, axis=0).transpose(1, 0, 2).reshape(1, tokens)
    dt_bc = jnp.take(dt_all.reshape(shards, heads, teams, quarter), order, axis=2)
    dt_bc = jnp.take(dt_bc, came, axis=0).transpose(1, 2, 0, 3).reshape(heads, tokens)
    dt_bc = jnp.concatenate([dt_bc, jnp.zeros((16 - heads, tokens), BF16)], axis=0)

    rate_here = lax.dynamic_slice_in_dim(decay_rate, me * width // head_dim, heads)
    rate_row = jnp.repeat(rate_here, width // heads)[None]
    rate_lane = jnp.concatenate([rate_here, jnp.zeros((128 - heads,), F32)])[None]

    x_all = exchange(by_channel(x_load))
    bc_ctx, dt_ctx = place(dest_bc, dt_bc, pieces, width, head_dim)
    dy_all = exchange(after(by_channel(grad_y), x_all))
    y_sent, y_all, x_ctx, states = fore(docs, destination, x_all, rate_row, bc_ctx, dt_ctx)
    y_got = exchange(after(y_sent, dy_all))
    dx_ctx, keep, give, ddt_ctx = back(
        docs, (team % 2)[None], rate_row, rate_lane, bc_ctx, dt_ctx, x_ctx, dy_all, y_all,
        states, head_dim,
    )
    more = across(give, 1)
    dx_sent = gather_back(destination, dx_ctx, shards)
    dx_got = exchange(after(dx_sent, y_got))
    cbits, hbits = shards.bit_length() - 1, teams.bit_length() - 1
    near = [("ctx", 1 << k) for k in reversed(range(cbits))]
    links = near + [("head", 1 << k) for k in reversed(range(1, hbits))]
    turns = sorted(links, key=lambda v: (v[0] == "ctx", v[1]))

    def bit_of(axis, reach):
        return (lax.axis_index(axis) // reach) % 2

    def swap(v, axis, reach):
        return lax.ppermute(v, axis, [(i, i ^ reach) for i in range(lax.axis_size(axis))])

    axis, reach = turns[0]
    at = links.index(turns[0])
    links.pop(at)
    spots = destination.reshape((2,) * (cbits + hbits - 1) + (2 * quarter,))
    bit = bit_of(axis, reach)
    kept_spots = lax.dynamic_index_in_dim(spots, bit, at, False)
    given_spots = lax.dynamic_index_in_dim(spots, 1 - bit, at, False)
    given = gather_rows(given_spots.reshape(-1), keep, more)
    came = swap(given, axis, reach)
    kept = gather_rows(kept_spots.reshape(-1), keep, more)
    part = (kept + came).reshape(kept_spots.shape + (128,))
    for axis, reach in turns[1:]:
        at = links.index((axis, reach))
        links.pop(at)
        bit = bit_of(axis, reach)
        give = lax.dynamic_index_in_dim(part, 1 - bit, at, False)
        part = lax.dynamic_index_in_dim(part, bit, at, False) + swap(give, axis, reach)
    part = part.astype(BF16)
    for reach in (1 << k for k in range(hbits)):
        other, first = across(part, reach), bit_of("head", reach) == 0
        low, high = jnp.where(first, part, other), jnp.where(first, other, part)
        part = jnp.concatenate([low, high], axis=1 if reach == 1 else 0)
    dbc_load = part

    ddt = gather_turn(destination, ddt_ctx, heads)[:heads]
    ddt = ddt.reshape(heads, shards, rows_dev).transpose(1, 0, 2)
    ddt = ddt if sharing > 1 else ddt.astype(BF16)
    ddt = ddt.reshape((2,) * cbits + (heads, rows_dev))
    for at, (axis, reach) in enumerate(near):
        bit = bit_of(axis, reach)
        stay = lax.dynamic_index_in_dim(ddt, bit, at, True)
        came = swap(lax.dynamic_index_in_dim(ddt, 1 - bit, at, True), axis, reach)
        low, high = jnp.where(bit == 0, stay, came), jnp.where(bit == 0, came, stay)
        ddt = jnp.concatenate([low, high], axis=at)
    ddt = jnp.sum(ddt.astype(F32).reshape(heads_dev, sharing, rows_dev), axis=1)
    return (from_channel(y_got), from_channel(dx_got), dbc_load, ddt.T.astype(BF16))


def inverse(order):
    teams = jnp.arange(order.shape[0], dtype=order.dtype)
    return jnp.argmax(order[None, :] == teams[:, None], axis=1)


def solution(mesh):
    return jax.shard_map(
        body,
        mesh=mesh,
        in_specs=(
            P("ctx", "head"),
            P("ctx", None),
            P("ctx", "head"),
            P("head"),
            P("ctx"),
            P(),
            P("ctx", "head"),
        ),
        out_specs=(P("ctx", "head"), P("ctx", "head"), P("ctx", None), P("ctx", "head")),
        check_vma=False,
    )
```

```python
import functools
import jax
import jax.numpy as jnp
from jax import lax
from jax.experimental import pallas as pl
from jax.experimental.pallas import tpu as pltpu
from jax.sharding import PartitionSpec as P


BLOCK = 256
PLACE = 1024
F32, BF16, I32 = jnp.float32, jnp.bfloat16, jnp.int32
NN, NT, TN = (((1,), (0,)), ((), ())), (((1,), (1,)), ((), ())), (((0,), (0,)), ((), ()))
VMEM = pl.BlockSpec(memory_space=pltpu.VMEM)
SMEM = pl.BlockSpec(memory_space=pltpu.SMEM)


def dot(a, b, dims=NN):
    return lax.dot_general(a, b, dims, preferred_element_type=F32)


def split2(v):
    hi = v.astype(BF16)
    return hi, (v - hi.astype(F32)).astype(BF16)


def expander(heads, width, head_dim):
    h = lax.broadcasted_iota(I32, (heads, width), 0)
    c = lax.broadcasted_iota(I32, (heads, width), 1)
    return jnp.where(c // head_dim == h, 1.0, 0.0).astype(BF16)


def place_kernel(pieces, head_dim, dest_ref, dt_ref, *refs):
    bc_refs, (bc_out, dt_out) = refs[:pieces], refs[pieces:]
    size = bc_refs[0].shape[0]
    block = bc_out.shape[0]
    first = pl.program_id(0) * block
    acc_bc = jnp.zeros((block, bc_out.shape[1]), F32)
    acc_dt = jnp.zeros((block, dt_ref.shape[0]), F32)
    for e in range(pieces):
        here = lax.broadcasted_iota(I32, (block, size), 0) + first
        pick = jnp.where(here == dest_ref[:, e * size : (e + 1) * size], 1.0, 0.0).astype(BF16)
        acc_bc = acc_bc + dot(pick, bc_refs[e][...])
        acc_dt = acc_dt + dot(pick, dt_ref[:, e * size : (e + 1) * size], NT)
    bc_out[...] = acc_bc.astype(BF16)
    spread = expander(dt_ref.shape[0], dt_out.shape[1], head_dim)
    dt_out[...] = dot(acc_dt.astype(BF16), spread).astype(BF16)


def constants(lower_ref, spread_ref, head_dim):
    rows = lax.broadcasted_iota(I32, (BLOCK, BLOCK), 0)
    cols = lax.broadcasted_iota(I32, (BLOCK, BLOCK), 1)
    lower_ref[...] = jnp.where(rows >= cols, 1.0, 0.0).astype(BF16)
    if spread_ref is not None:
        width = spread_ref.shape[0] // 2
        c = lax.broadcasted_iota(I32, (width, 128), 0)
        h = lax.broadcasted_iota(I32, (width, 128), 1)
        one = jnp.where(c // head_dim == h, 1.0, 0.0).astype(BF16)
        spread_ref[...] = jnp.concatenate([one] * 2, axis=0)


def decays(dt_ref, rate_ref, lower_ref):
    running = rate_ref[...] * dot(lower_ref[...], dt_ref[...])
    return jnp.exp(-running), jnp.exp(running), jnp.exp(-running[BLOCK - 1 :, :])


def doc_state(doc_smem, block):
    last = doc_smem[block * BLOCK + BLOCK - 1]
    prev = jnp.where(block == 0, -1.0, doc_smem[jnp.maximum(block * BLOCK - 1, 0)])
    return prev, last


def only(cond, v):
    return jnp.where(cond, v.astype(F32), 0.0).astype(BF16)


def lanes(*parts):
    return jnp.concatenate(parts, axis=1)


def stack(*parts):
    return jnp.concatenate(parts, axis=0)


def fore_kernel(
    doc_smem, doc_ref, doc_col, dest_ref, x_ref, rate_ref, bc_ref, dt_ref,
    y_out, yf_out, x_out, state_out, state_ref, lower_ref,
):
    block = pl.program_id(0)

    @pl.when(block == 0)
    def _():
        state_ref[...] = jnp.zeros_like(state_ref)
        constants(lower_ref, None, None)

    tokens = x_ref.shape[0]
    here = lax.broadcasted_iota(I32, (BLOCK, tokens), 0) + block * BLOCK
    pick = jnp.where(here == dest_ref[...], 1.0, 0.0).astype(BF16)
    x = dot(pick, x_ref[...])
    x_out[...] = x.astype(BF16)
    b, c = bc_ref[:, :128], bc_ref[:, 128:]
    enter, leave, total = decays(dt_ref, rate_ref, lower_ref)
    prev, last = doc_state(doc_smem, block)
    row, col = doc_ref[...], doc_col[...]
    rows = lax.broadcasted_iota(I32, (BLOCK, BLOCK), 0)
    cols = lax.broadcasted_iota(I32, (BLOCK, BLOCK), 1)
    earlier = (col == row) & (rows >= cols)
    ah, al = split2(jnp.where(earlier, dot(c, b, NT), 0.0))
    uh, ul = split2(leave * (dt_ref[...].astype(F32) * x))
    state = state_ref[...]
    state_out[0] = state
    sh, sl = split2(state)
    c_first = only(col == prev, c)
    y = enter * dot(lanes(ah, ah, al, c_first, c_first), stack(uh, ul, uh, sh, sl))
    yf_out[...] = y
    y_out[...] = y.astype(BF16)
    b_last = only(col == last, b)
    fresh = dot(stack(b_last, b_last), stack(uh, ul), TN)
    state_ref[...] = total * (jnp.where(prev == last, state, 0.0) + fresh)


def back_kernel(
    blocks, head_dim, pieces, slot_smem, doc_smem, side_smem, doc_ref, doc_col, rate_ref, rate_lane,
    bc_ref, dt_ref, x_ref, y_ref, state_ref, *refs,
):
    dy_refs = refs[:pieces]
    dx_out, keep_out, give_out, ddt_out = refs[pieces : pieces + 4]
    dy_ref, grad_ref, sum_ref, lower_ref, spread_ref = refs[pieces + 4 :]
    step = pl.program_id(0)
    each = blocks // pieces
    slot = slot_smem[(blocks - 1 - step) // each]
    for e in range(pieces):

        @pl.when(slot == e)
        def _(e=e):
            at = ((blocks - 1 - step) % each) * BLOCK
            dy_ref[...] = dy_refs[e][pl.ds(pl.multiple_of(at, BLOCK), BLOCK), :]

    @pl.when(step == 0)
    def _():
        grad_ref[...] = jnp.zeros_like(grad_ref)
        sum_ref[...] = jnp.zeros_like(sum_ref)
        constants(lower_ref, spread_ref, head_dim)

    block = blocks - 1 - step
    b, c = bc_ref[:, :128], bc_ref[:, 128:]
    enter, leave, total = decays(dt_ref, rate_ref, lower_ref)
    prev, last = doc_state(doc_smem, block)
    row, col = doc_ref[...], doc_col[...]
    rows = lax.broadcasted_iota(I32, (BLOCK, BLOCK), 0)
    cols = lax.broadcasted_iota(I32, (BLOCK, BLOCK), 1)
    later = (col == row) & (cols >= rows)
    is_last, is_first = col == last, col == prev
    ah, al = split2(jnp.where(later, dot(b, c, NT), 0.0))
    dt = dt_ref[...].astype(F32)
    x = x_ref[...].astype(F32)
    dy = dy_ref[...].astype(F32)
    gh, gl = split2(enter * dy)
    uh, ul = split2(leave * (dt * x))
    grad = total * grad_ref[...]
    rh, rl = split2(grad)
    sh, sl = split2(state_ref[0])
    b_last, c_first = only(is_last, b), only(is_first, c)
    du = leave * dot(lanes(ah, ah, al, b_last, b_last), stack(gh, gl, gh, rh, rl))
    dx = dt * du
    dx_out[...] = dx.astype(BF16)
    fresh = dot(stack(c_first, c_first), stack(gh, gl), TN)
    grad_ref[...] = jnp.where(prev == last, grad, 0.0) + fresh
    g3, u3 = lanes(gh, gl, gh), lanes(uh, uh, ul)
    qh, qlow = split2(jnp.where(later, dot(u3, g3, NT), 0.0))
    dc = dot(stack(qh, qlow), stack(b, b), TN)
    dc = dc + jnp.where(is_first, dot(g3, lanes(sh, sh, sl), NT), 0.0)
    db = dot(lanes(qh, qlow), stack(c, c))
    db = db + jnp.where(is_last, dot(u3, lanes(rh, rl, rh), NT), 0.0)
    side = side_smem[0] == 0
    keep_out[...] = jnp.where(side, db, dc)
    give_out[...] = jnp.where(side, dc, db)
    spread = spread_ref[...]
    balance = dot(lanes(*split2(dy * y_ref[...] - x * dx)), spread)
    mask = jnp.where(later, 1.0, 0.0).astype(BF16)
    suffix = dot(lanes(mask, mask), stack(*split2(balance)))
    suffix = suffix + jnp.where(is_last, sum_ref[:1, :], 0.0)
    sum_ref[...] = jnp.broadcast_to(
        jnp.where(prev == doc_smem[block * BLOCK], suffix[:1, :], 0.0), sum_ref.shape
    )
    ddt_out[...] = dot(lanes(*split2(x * du)), spread) - rate_lane[...] * suffix


def pick8(dest_smem, source, target, base):
    def rows8(i, carry):
        at = pl.multiple_of(i * 8, 8)
        spots = [dest_smem[base + at + j] for j in range(8)]
        target[pl.ds(at, 8), :] = stack(*[source[pl.ds(s, 1), :] for s in spots])
        return carry

    lax.fori_loop(0, target.shape[0] // 8, rows8, 0, unroll=4)


def rows_kernel(dest_smem, keep_ref, more_ref, dbc_out, sum_ref):
    sum_ref[...] = keep_ref[...] + more_ref[...]
    pick8(dest_smem, sum_ref, dbc_out, 0)


def turn_kernel(dest_smem, ddt_ref, ddt_out, small_ref):
    pick8(dest_smem, ddt_ref, small_ref, pl.program_id(0) * BLOCK)
    ddt_out[...] = small_ref[...].T[: ddt_out.shape[0], :]


def gather_kernel(dest_col, dx_ref, dx_out):
    here = lax.broadcasted_iota(I32, (dx_out.shape[0], dx_ref.shape[0]), 1)
    pick = jnp.where(here == dest_col[...], 1.0, 0.0).astype(BF16)
    dx_out[...] = dot(pick, dx_ref[...]).astype(BF16)


def params(**extra):
    return pltpu.CompilerParams(
        dimension_semantics=("arbitrary",), vmem_limit_bytes=60 << 20, **extra
    )


def struct(dtype, *shape):
    return jax.ShapeDtypeStruct(shape, dtype)


def blocked(cols, index, size=BLOCK):
    return pl.BlockSpec((size, cols), lambda s, *more: (index(s), 0))


def rowed(rows, index):
    return pl.BlockSpec((rows, BLOCK), lambda s, *more: (0, index(s)))


def planes(width, index):
    return pl.BlockSpec((1, 128, width), lambda s, *more: (index(s), 0, 0))


def place(dest_bc, dt_bc, pieces, width, head_dim):
    tokens = dest_bc.shape[1]
    same = lambda s: s
    return pl.pallas_call(
        functools.partial(place_kernel, len(pieces), head_dim),
        grid=(tokens // PLACE,),
        in_specs=[VMEM] * (2 + len(pieces)),
        out_specs=[blocked(256, same, PLACE), blocked(width, same, PLACE)],
        out_shape=[struct(BF16, tokens, 256), struct(BF16, tokens, width)],
        compiler_params=params(),
        cost_estimate=pl.CostEstimate(
            flops=2 * tokens * tokens * 384, bytes_accessed=tokens * 1600, transcendentals=0
        ),
        name="place",
    )(dest_bc, dt_bc, *pieces)


def fore(docs, destination, x_all, rate_row, bc_ctx, dt_ctx):
    tokens, width = x_all.shape
    blocks = tokens // BLOCK
    same = lambda s: s
    return pl.pallas_call(
        fore_kernel,
        grid=(blocks,),
        in_specs=[
            SMEM, rowed(1, same), blocked(1, same), VMEM, VMEM, VMEM,
            blocked(256, same), blocked(width, same),
        ],
        out_specs=[blocked(width, same)] * 3 + [planes(width, same)],
        out_shape=[
            struct(BF16, tokens, width),
            struct(F32, tokens, width),
            struct(BF16, tokens, width),
            struct(F32, blocks, 128, width),
        ],
        scratch_shapes=[pltpu.VMEM((128, width), F32), pltpu.VMEM((BLOCK, BLOCK), BF16)],
        compiler_params=params(),
        cost_estimate=pl.CostEstimate(
            flops=2 * tokens * (tokens + 2000) * width,
            bytes_accessed=tokens * 4000,
            transcendentals=2 * tokens * width,
        ),
        name="fore",
    )(docs, docs[None], docs[:, None], destination[None], x_all, rate_row, bc_ctx, dt_ctx)


def back(slots, docs, side, rate_row, rate_lane, bc_ctx, dt_ctx, x_ctx, dy_all, y_all, states, head_dim):
    tokens, width = x_ctx.shape
    blocks = tokens // BLOCK
    down = lambda s: blocks - 1 - s
    return pl.pallas_call(
        functools.partial(back_kernel, blocks, head_dim, len(dy_all)),
        grid_spec=pltpu.PrefetchScalarGridSpec(
            num_scalar_prefetch=1,
            grid=(blocks,),
            in_specs=[
                SMEM, SMEM, rowed(1, down), blocked(1, down), VMEM, VMEM,
                blocked(256, down), blocked(width, down), blocked(width, down),
                blocked(width, down), planes(width, down),
            ] + [VMEM] * len(dy_all),
            out_specs=[blocked(width, down)] + [blocked(128, down)] * 3,
            scratch_shapes=[
                pltpu.VMEM((BLOCK, width), BF16),
                pltpu.VMEM((128, width), F32),
                pltpu.VMEM((8, 128), F32),
                pltpu.VMEM((BLOCK, BLOCK), BF16),
                pltpu.VMEM((2 * width, 128), BF16),
            ],
        ),
        out_shape=[struct(BF16, tokens, width)] + [struct(F32, tokens, 128)] * 3,
        compiler_params=params(),
        cost_estimate=pl.CostEstimate(
            flops=2 * tokens * 4000 * width,
            bytes_accessed=tokens * 6000,
            transcendentals=2 * tokens * width,
        ),
        name="back",
    )(
        slots, docs, side, docs[None], docs[:, None], rate_row, rate_lane,
        bc_ctx, dt_ctx, x_ctx, y_all, states, *dy_all,
    )


def gather_rows(spots, keep, more):
    return pl.pallas_call(
        rows_kernel,
        in_specs=[SMEM, VMEM, VMEM],
        out_specs=VMEM,
        out_shape=struct(F32, spots.shape[0], 128),
        scratch_shapes=[pltpu.VMEM(keep.shape, F32)],
        compiler_params=pltpu.CompilerParams(vmem_limit_bytes=60 << 20),
        cost_estimate=pl.CostEstimate(
            flops=keep.size, bytes_accessed=keep.size * 12, transcendentals=0
        ),
        name="gather_rows",
    )(spots, keep, more)


def gather_turn(destination, ddt, heads):
    tokens = ddt.shape[0]
    padded = -(-heads // 8) * 8
    return pl.pallas_call(
        turn_kernel,
        grid=(tokens // BLOCK,),
        in_specs=[SMEM, VMEM],
        out_specs=rowed(padded, lambda s: s),
        out_shape=struct(F32, padded, tokens),
        scratch_shapes=[pltpu.VMEM((BLOCK, 128), F32)],
        compiler_params=params(),
        cost_estimate=pl.CostEstimate(
            flops=tokens * 256, bytes_accessed=tokens * 1000, transcendentals=0
        ),
        name="gather_turn",
    )(destination, ddt)


def gather_back(destination, dx_ctx, shards):
    tokens, width = dx_ctx.shape
    size = tokens // shards
    return pl.pallas_call(
        gather_kernel,
        grid=(shards,),
        in_specs=[blocked(1, lambda s: s, size), VMEM],
        out_specs=blocked(width, lambda s: s, size),
        out_shape=struct(BF16, tokens, width),
        compiler_params=params(),
        cost_estimate=pl.CostEstimate(
            flops=2 * tokens * tokens * width, bytes_accessed=tokens * 1500, transcendentals=0
        ),
        name="gather_back",
    )(destination[:, None], dx_ctx)


def after(value, *others):
    return lax.optimization_barrier((value,) + others)[0]


def body(x_load, bc_load, dt_load, decay_rate, doc_ids, destination, grad_y):
    shards, teams = lax.axis_size("ctx"), lax.axis_size("head")
    me, team = lax.axis_index("ctx"), lax.axis_index("head")
    rows_dev, chan_dev = x_load.shape
    heads_dev = dt_load.shape[1]
    head_dim = chan_dev // heads_dev
    width = chan_dev // shards
    tokens = rows_dev * shards
    heads = max(1, width // head_dim)
    sharing = shards * heads // heads_dev
    quarter = rows_dev // teams

    def exchange(v):
        return lax.all_to_all(v, "ctx", split_axis=0, concat_axis=0, tiled=True)

    def ring(v, reach):
        return lax.ppermute(v, "ctx", [(i, i ^ reach) for i in range(shards)])

    def across(v, reach):
        return lax.ppermute(v, "head", [(i, i ^ reach) for i in range(teams)])

    def by_channel(v):
        parts = v.reshape(rows_dev, shards, width).transpose(1, 0, 2)
        return parts.reshape(tokens, width)

    def from_channel(got):
        got = got.reshape(shards, rows_dev, width)
        return got.transpose(1, 0, 2).reshape(rows_dev, chan_dev)

    own_bc = lax.dynamic_slice_in_dim(bc_load, team * quarter, quarter)
    small = jnp.concatenate([dt_load.T, doc_ids.astype(BF16)[None]], axis=0)
    extra = small.size // 256
    fill = jnp.zeros((-extra % 16, 256), BF16)
    held = jnp.concatenate([own_bc, small.reshape(-1, 256), fill], axis=0)[None]
    came, reach, early = [me], shards // 2, None
    while reach >= 1:
        held = jnp.concatenate([held, ring(held, reach)], axis=0)
        came = came + [t ^ reach for t in came]
        early = held if reach > 1 else early
        reach //= 2
    came = jnp.stack(came)
    part_bc = held[:, :quarter].reshape(shards * quarter, 256)
    small = jnp.take(held[:, quarter : quarter + extra], inverse(came), axis=0)
    small = small.reshape(shards, heads_dev + 1, rows_dev)
    docs = small[:, heads_dev].astype(F32).reshape(tokens)
    dt_all = lax.dynamic_slice_in_dim(small, me * width // head_dim, heads, axis=1)
    pieces, order, reach = [part_bc], [team], teams // 2
    while reach >= 1:
        pieces = pieces + [across(v, reach) for v in pieces]
        order = order + [t ^ reach for t in order]
        reach //= 2
    order = jnp.stack(order)
    dest_bc = jnp.take(destination.reshape(shards, teams, quarter), order, axis=1)
    dest_bc = jnp.take(dest_bc, came, axis=0).transpose(1, 0, 2).reshape(1, tokens)
    dt_bc = jnp.take(dt_all.reshape(shards, heads, teams, quarter), order, axis=2)
    dt_bc = jnp.take(dt_bc, came, axis=0).transpose(1, 2, 0, 3).reshape(heads, tokens)
    dt_bc = jnp.concatenate([dt_bc, jnp.zeros((16 - heads, tokens), BF16)], axis=0)

    rate_here = lax.dynamic_slice_in_dim(decay_rate, me * width // head_dim, heads)
    rate_row = jnp.repeat(rate_here, width // heads)[None]
    rate_lane = jnp.concatenate([rate_here, jnp.zeros((128 - heads,), F32)])[None]

    x_all = exchange(by_channel(x_load))
    bc_ctx, dt_ctx = place(dest_bc, dt_bc, pieces, width, head_dim)
    slots = jnp.arange(shards, dtype=I32) ^ me
    parts = grad_y.reshape(rows_dev, shards, width).transpose(1, 0, 2)
    late = me + jnp.where(early[-1, quarter + extra - 1, -1] < 0, 1, 0)
    dy_all = []
    for e in range(shards):
        piece = lax.dynamic_index_in_dim(parts, late ^ e, 0, False)
        dy_all.append(ring(piece, e) if e else piece)
    y_sent, y_all, x_ctx, states = fore(docs, destination, x_all, rate_row, bc_ctx, dt_ctx)
    y_got = exchange(y_sent)
    dx_ctx, keep, give, ddt_ctx = back(
        slots, docs, (team % 2)[None], rate_row, rate_lane, bc_ctx, dt_ctx, x_ctx, dy_all, y_all,
        states, head_dim,
    )
    more = across(give, 1)
    dx_sent = gather_back(destination, dx_ctx, shards)
    dx_got = exchange(after(dx_sent, y_got))
    cbits, hbits = shards.bit_length() - 1, teams.bit_length() - 1
    near = [("ctx", 1 << k) for k in reversed(range(cbits))]
    links = near + [("head", 1 << k) for k in reversed(range(1, hbits))]
    turns = sorted(links, key=lambda v: (v[0] == "ctx", v[1]))

    def bit_of(axis, reach):
        return (lax.axis_index(axis) // reach) % 2

    def swap(v, axis, reach):
        return lax.ppermute(v, axis, [(i, i ^ reach) for i in range(lax.axis_size(axis))])

    axis, reach = turns[0]
    at = links.index(turns[0])
    links.pop(at)
    spots = destination.reshape((2,) * (cbits + hbits - 1) + (2 * quarter,))
    bit = bit_of(axis, reach)
    kept_spots = lax.dynamic_index_in_dim(spots, bit, at, False)
    given_spots = lax.dynamic_index_in_dim(spots, 1 - bit, at, False)
    given = gather_rows(given_spots.reshape(-1), keep, more)
    came = swap(given, axis, reach)
    kept = gather_rows(kept_spots.reshape(-1), keep, more)
    part = (kept + came).reshape(kept_spots.shape + (128,))
    for axis, reach in turns[1:]:
        at = links.index((axis, reach))
        links.pop(at)
        bit = bit_of(axis, reach)
        give = lax.dynamic_index_in_dim(part, 1 - bit, at, False)
        part = lax.dynamic_index_in_dim(part, bit, at, False) + swap(give, axis, reach)
    part = part.astype(BF16)
    for reach in (1 << k for k in range(hbits)):
        other, first = across(part, reach), bit_of("head", reach) == 0
        low, high = jnp.where(first, part, other), jnp.where(first, other, part)
        part = jnp.concatenate([low, high], axis=1 if reach == 1 else 0)
    dbc_load = part

    ddt = gather_turn(destination, ddt_ctx, heads)[:heads]
    ddt = ddt.reshape(heads, shards, rows_dev).transpose(1, 0, 2)
    ddt = ddt if sharing > 1 else ddt.astype(BF16)
    ddt = ddt.reshape((2,) * cbits + (heads, rows_dev))
    for at, (axis, reach) in enumerate(near):
        bit = bit_of(axis, reach)
        stay = lax.dynamic_index_in_dim(ddt, bit, at, True)
        came = swap(lax.dynamic_index_in_dim(ddt, 1 - bit, at, True), axis, reach)
        low, high = jnp.where(bit == 0, stay, came), jnp.where(bit == 0, came, stay)
        ddt = jnp.concatenate([low, high], axis=at)
    ddt = jnp.sum(ddt.astype(F32).reshape(heads_dev, sharing, rows_dev), axis=1)
    return (from_channel(y_got), from_channel(dx_got), dbc_load, ddt.T.astype(BF16))


def inverse(order):
    teams = jnp.arange(order.shape[0], dtype=order.dtype)
    return jnp.argmax(order[None, :] == teams[:, None], axis=1)


def solution(mesh):
    return jax.shard_map(
        body,
        mesh=mesh,
        in_specs=(
            P("ctx", "head"),
            P("ctx", None),
            P("ctx", "head"),
            P("head"),
            P("ctx"),
            P(),
            P("ctx", "head"),
        ),
        out_specs=(P("ctx", "head"), P("ctx", "head"), P("ctx", None), P("ctx", "head")),
        check_vma=False,
    )
```
